512 devices in a mesh: section: 8 (over x, core), dp: 4 (over z_lo), tensor: 16 (over z_hi, y).
Axes of the slice: x: 4, y: 4, z: 16 (z_hi: 4, z_lo: 4; z = z_hi * 4 + z_lo), core: 2. Of those that a mesh axis runs over, the one named last changes fastest.
Arguments:
- section_input: bfloat16 [8, 4, 256, 4096], P('section', 'dp', 'tensor'), may hold values from -6 to 6
- carried_grad: bfloat16 [8, 4, 256, 4096], P('section', 'dp', 'tensor'), may hold values from -6 to 6
- hidden_grad: bfloat16 [8, 4, 256, 14336], P('section', 'dp', None, 'tensor'), may hold values from -6 to 6
- saved_gate: bfloat16 [8, 4, 256, 14336], P('section', 'dp', None, 'tensor'), may hold values from -8 to 8
- w_up: bfloat16 [8, 4096, 14336], P('section', 'dp', 'tensor'), may hold values from -0.09375 to 0.09375
Outputs:
- passed_grad: bfloat16 [8, 4, 256, 4096], P('section', 'dp', 'tensor')
- up_weight_grad: bfloat16 [8, 4096, 14336], P('section', 'dp', 'tensor')
The draws below stay inside these ranges and needn't reach their ends.
All inputs are finite; a program needn't handle non-finite values.
Results may differ from the reference program's by a relative error of at most 0.015.
Values may be sent and summed in bfloat16 or wider, within the bound.
A program may use at most 64 MiB of HBM per device.

```python
import jax
import jax.numpy as jnp
from jax import lax

D = 4096
TOK = 256
FF = 14336
SECTIONS = 8
REPLICAS = 4
N_TENSOR = 16


def strengthened(result, rng, source, target, blocks, factor):
    owner, partner = [(jnp.arange(result.shape[position]) // (result.shape[position] // blocks)).reshape([-1 if axis == position else 1 for axis in range(result.ndim)]) for position in (source, target)]
    chosen = jax.random.permutation(rng, blocks)[partner]
    strong = (owner == chosen) | (owner == (partner + blocks // 2) % blocks)
    return jnp.where(strong, factor * result, result)


def steps_of(key, dims, pieces, least, top_value):
    loudness = 1.0
    for dim, shards_of in pieces:
        heights = jax.random.uniform(jax.random.fold_in(jax.random.fold_in(key, 6), dim), (shards_of,), jnp.float32, least / len(pieces), top_value / len(pieces))
        loudness = loudness * jnp.repeat(jnp.exp(heights), dims[dim] // shards_of).reshape((-1,) + (1,) * (len(dims) - 1 - dim))
    return loudness


def gaussian(key, shape, deviation, reach, pieces=(), held_as=jnp.bfloat16):
    factor_of = steps_of(key, shape, pieces, -0.22, 0.18) if pieces else 1.0
    entries = jax.random.normal(key, shape, jnp.float32) * deviation * factor_of
    return jnp.minimum(jnp.maximum(entries, -reach), reach).astype(held_as)


def gaussian_with(key, shape, deviation, most, cuts, heavy, dtype=jnp.bfloat16):
    drawn = deviation * jax.random.normal(key, shape, jnp.float32)
    if cuts:
        drawn = drawn * steps_of(key, shape, cuts, -0.22, 0.18)
    return jnp.clip(strengthened(drawn, jax.random.fold_in(key, 3), *heavy), -most, most).astype(dtype)


def setup_inputs(seed: int = 0) -> dict:
    streams_of = jax.random.split(jax.random.key(seed), 6)
    return {
        "section_input": gaussian(streams_of[0], (SECTIONS, REPLICAS, TOK, D), 1.0, 6.0, ((0, 8), (1, 4), (2, 16))),
        "carried_grad": gaussian(streams_of[1], (SECTIONS, REPLICAS, TOK, D), 1.0, 6.0, ((0, 8), (1, 4), (2, 16))),
        "hidden_grad": gaussian_with(streams_of[2], (SECTIONS, REPLICAS, TOK, FF), 1.0, 6.0, ((0, 8), (1, 4), (3, 16)), (3, 2, 16, 2.0)),
        "saved_gate": gaussian(streams_of[3], (SECTIONS, REPLICAS, TOK, FF), 1.5, 8.0, ((0, 8), (1, 4), (3, 16))),
        "w_up": gaussian(streams_of[4], (SECTIONS, D, FF), D ** -0.5, 0.09375, ((0, 8), (1, 4), (2, 16))),
    }


def section_backward(item):
    inputs, carried, grads, gates, up_weight = item
    width = up_weight.shape[0]

    def one_replica(rep):
        carried_rows, grad_rows, gate_rows = rep
        gate = gate_rows.astype(jnp.float32)
        sig = jax.nn.sigmoid(gate)
        up_grad = (grad_rows.astype(jnp.float32) * gate * sig).astype(jnp.bfloat16)
        tokens = up_grad.shape[0]
        up_blocks = up_grad.reshape(tokens, N_TENSOR, -1).astype(jnp.float32)
        weight_blocks = up_weight.reshape(width, N_TENSOR, -1).astype(jnp.float32)
        parts = jnp.einsum('tnf,dnf->ntd', up_blocks, weight_blocks)
        parts = lax.optimization_barrier(parts.astype(jnp.bfloat16)).astype(jnp.float32)
        input_grad = (jnp.sum(parts, axis=0) + carried_rows.astype(jnp.float32)).astype(jnp.bfloat16)
        return input_grad, up_grad

    input_grad, up_grad = lax.map(one_replica, (carried, grads, gates))
    weight_grad = jnp.dot(inputs.reshape(-1, width).T, up_grad.reshape(-1, up_grad.shape[-1]), preferred_element_type=jnp.float32)
    return input_grad, (weight_grad / inputs.shape[0]).astype(jnp.bfloat16)


def reference(section_input, carried_grad, hidden_grad, saved_gate, w_up):
    input_grad, up_weight_grad = lax.map(section_backward, (section_input, carried_grad, hidden_grad, saved_gate, w_up))
    passed_grad = jnp.concatenate([input_grad[1:], jnp.zeros_like(input_grad[:1])], axis=0)
    return passed_grad, up_weight_grad
```

```python
import functools

import jax
import jax.numpy as jnp
from jax import lax
from jax.experimental import pallas as pl
from jax.experimental.pallas import tpu as pltpu
from jax.sharding import PartitionSpec as P

MESH = pl.DeviceIdType.MESH
R = 4
H = 4
Y = 4
CHUNKS = 2


def block_at(position, step):
    near = jnp.minimum(position, R - 1 - position)
    low = jnp.where((near == 1) & (step < 2), 1 - step, step)
    return jnp.where(position < 2, low, R - 1 - low)


def kernel(
    x_in, carried, grads, gates, w,
    passed, weight_grad,
    up, part, from_y, total, from_z, x, carry,
    up_send, up_recv, xz_send, xz_recv, xy_send, xy_recv,
    py_send, py_recv, pz_send, pz_recv, carry_send, carry_recv,
):
    section = lax.axis_index("section")
    sections = lax.axis_size("section")
    dp = lax.axis_index("dp")
    tensor = lax.axis_index("tensor")
    hi = tensor // Y
    y = lax.rem(tensor, Y)
    z = hi * R + dp
    tokens, hidden = grads.shape
    rows = x_in.shape[0]
    cols = w.shape[0]
    piece = tokens // CHUNKS

    def at(sec, r, h, yy):
        return {"section": sec, "dp": r, "tensor": h * Y + yy}

    def remote(src, dst, send, recv, device):
        return pltpu.make_async_remote_copy(
            src_ref=src, dst_ref=dst, send_sem=send, recv_sem=recv, device_id=device, device_id_type=MESH
        )

    barrier = pltpu.get_barrier_semaphore()

    def greet(k, _):
        other = lax.rem(z + k, R * H)
        pl.semaphore_signal(
            barrier, inc=1, device_id=at(section, lax.rem(other, R), other // R, y), device_id_type=MESH
        )
        return 0

    lax.fori_loop(1, R * H, greet, 0)
    for k in range(1, Y):
        pl.semaphore_signal(
            barrier, inc=1, device_id=at(section, dp, hi, lax.rem(y + k, Y)), device_id_type=MESH
        )

    @pl.when(section < sections - 1)
    def _():
        def greet_next(other, _):
            pl.semaphore_signal(
                barrier, inc=1, device_id=at(section + 1, lax.rem(other, R), other // R, y), device_id_type=MESH
            )
            return 0

        lax.fori_loop(0, R * H, greet_next, 0)

    def activate(i, _):
        at_rows = pl.ds(pl.multiple_of(i * 64, 64), 64)
        gate = gates[at_rows, :].astype(jnp.float32)
        value = grads[at_rows, :].astype(jnp.float32) * gate * jax.nn.sigmoid(gate)
        up[dp, at_rows, :] = value.astype(jnp.bfloat16)
        return 0

    lax.fori_loop(0, tokens // 64, activate, 0)
    x[dp, hi, y] = x_in[:, pl.ds(pl.multiple_of(dp * cols, cols), cols)]

    pl.semaphore_wait(barrier, R * H - 1 + Y - 1 + R * H * jnp.minimum(section, 1))

    def up_copy(o, c, way):
        ref = up.at[o, pl.ds(c * piece, piece)]
        return remote(
            ref, ref, up_send.at[way, o, c], up_recv.at[o, c],
            at(section, jnp.clip(dp + (1 if way == 1 else -1), 0, R - 1), hi, y),
        )

    def to_right(o):
        return (dp < R - 1) & (o <= dp)

    def to_left(o):
        return (dp > 0) & (o >= dp)

    def pass_on(o, c):
        @pl.when(to_right(o))
        def _():
            up_copy(o, c, 1).start()

        @pl.when(to_left(o))
        def _():
            up_copy(o, c, 0).start()

    def carry_copy():
        return remote(carried, carry, carry_send, carry_recv, at(jnp.maximum(section - 1, 0), dp, hi, y))

    def part_copy(o, k):
        peer = lax.rem(y + k, Y)
        return remote(
            part.at[o, :, peer], from_y.at[k - 1, o], py_send.at[k - 1, o], py_recv.at[k - 1, o],
            at(section, dp, hi, peer),
        )

    def multiply(step, _):
        o = block_at(dp, step)
        for c in range(CHUNKS):

            @pl.when(step > 0)
            def _():
                up_copy(o, c, 0).wait_recv()

            pass_on(o, c)

        def tile(n, _):
            at_cols = pl.ds(pl.multiple_of(n * 256, 256), 256)
            out = lax.dot_general(
                up[o], w[at_cols, :], (((1,), (1,)), ((), ())), preferred_element_type=jnp.float32
            )
            part[o, :, :, :, at_cols] = out.astype(jnp.bfloat16).reshape(H, Y, rows, 256)
            return 0

        lax.fori_loop(0, cols // 256, tile, 0)
        for k in (1, 3, 2):
            part_copy(o, k).start()
        return 0

    lax.fori_loop(0, R, multiply, 0)

    def xz_copy(k):
        other = lax.rem(z + k, R * H)
        d = lax.rem(other, R)
        return remote(
            x_in.at[:, pl.ds(pl.multiple_of(d * cols, cols), cols)], x.at[dp, hi, y],
            xz_send.at[k], xz_recv.at[k], at(section, d, other // R, y),
        )

    def send_x(i, _):
        half = i // 2
        xz_copy(jnp.where(lax.rem(i, 2) == 0, half + 1, R * H - 1 - half)).start()
        return 0

    lax.fori_loop(0, R * H - 1, send_x, 0)

    @pl.when(section > 0)
    def _():
        carry_copy().start()

    def total_copy(o, h):
        return remote(
            total.at[o, h], from_z.at[z], pz_send.at[o, h], pz_recv.at[z],
            at(jnp.maximum(section - 1, 0), o, h, y),
        )

    def add_up(step, _):
        o = block_at(dp, step)
        for k in range(1, Y):
            part_copy(o, k).wait_recv()
        for h in range(H):
            value = part[o, h, y].astype(jnp.float32)
            for k in range(1, Y):
                value = value + from_y[k - 1, o, h].astype(jnp.float32)
            total[o, h] = value.astype(jnp.bfloat16)

        @pl.when(section > 0)
        def _():
            for h in range(H):
                total_copy(o, h).start()

        return 0

    lax.fori_loop(0, R, add_up, 0)

    def wait_x(k, _):
        xz_copy(k).wait_recv()
        return 0

    lax.fori_loop(1, R * H, wait_x, 0)

    def xy_copy(k):
        mine = x.at[:, :, y]
        return remote(
            mine, mine, xy_send.at[k - 1], xy_recv.at[k - 1], at(section, dp, hi, lax.rem(y + k, Y))
        )

    for k in (1, 3, 2):
        xy_copy(k).start()
    for k in (1, 3, 2):
        xy_copy(k).wait_recv()

    up_all = up.reshape(R * tokens, hidden)

    def weight_tile(n, _):
        at_cols = pl.ds(pl.multiple_of(n * 256, 256), 256)
        xs = x[:, :, :, :, at_cols].reshape(R * tokens, 256)
        out = lax.dot_general(
            xs, up_all[...], (((0,), (0,)), ((), ())), preferred_element_type=jnp.float32
        )
        weight_grad[pl.ds(pl.multiple_of(n * 256, 256), 256), :] = (out * (1.0 / R)).astype(jnp.bfloat16)
        return 0

    lax.fori_loop(0, cols // 256, weight_tile, 0)

    @pl.when(section < sections - 1)
    def _():
        carry_copy().wait_recv()

        def wait_total(other, _):
            remote(
                total.at[0, 0], from_z.at[other], pz_send.at[0, 0], pz_recv.at[other],
                at(jnp.maximum(section - 1, 0), dp, hi, y),
            ).wait_recv()
            return 0

        lax.fori_loop(0, R * H, wait_total, 0)
        for d in range(R):
            at_cols = pl.ds(d * cols, cols)
            value = from_z[d].astype(jnp.float32)
            for h in range(1, H):
                value = value + from_z[h * R + d].astype(jnp.float32)
            passed[:, at_cols] = (carry[:, at_cols].astype(jnp.float32) + value).astype(jnp.bfloat16)

    @pl.when(section == sections - 1)
    def _():
        passed[...] = jnp.zeros_like(passed)

    @pl.when(section > 0)
    def _():
        carry_copy().wait_send()
        for o in range(R):
            for h in range(H):
                total_copy(o, h).wait_send()

    def sent(o, _):
        for c in range(CHUNKS):

            @pl.when(to_right(o))
            def _():
                up_copy(o, c, 1).wait_send()

            @pl.when(to_left(o))
            def _():
                up_copy(o, c, 0).wait_send()

        for k in range(1, Y):
            part_copy(o, k).wait_send()
        return 0

    lax.fori_loop(0, R, sent, 0)

    def sent_x(k, _):
        xz_copy(k).wait_send()
        return 0

    lax.fori_loop(1, R * H, sent_x, 0)
    for k in range(1, Y):
        xy_copy(k).wait_send()


def body(section_input, carried_grad, hidden_grad, saved_gate, w_up):
    rows, width = section_input.shape[2:]
    tokens, hidden = hidden_grad.shape[2:]
    cols = w_up.shape[1]
    low = jnp.bfloat16
    dma = pltpu.SemaphoreType.DMA
    vmem = pl.BlockSpec(memory_space=pltpu.VMEM)
    passed, weight_grad = pl.pallas_call(
        kernel,
        out_shape=(jax.ShapeDtypeStruct((rows, width), low), jax.ShapeDtypeStruct((cols, hidden), low)),
        in_specs=[vmem] * 5,
        out_specs=(vmem, vmem),
        scratch_shapes=[
            pltpu.VMEM((R, tokens, hidden), low),
            pltpu.VMEM((R, H, Y, rows, cols), low),
            pltpu.VMEM((Y - 1, R, H, rows, cols), low),
            pltpu.VMEM((R, H, rows, cols), low),
            pltpu.VMEM((R * H, rows, cols), low),
            pltpu.VMEM((R, H, Y, rows, cols), low),
            pltpu.VMEM((rows, width), low),
            dma((2, R, CHUNKS)), dma((R, CHUNKS)),
            dma((R * H,)), dma((R * H,)),
            dma((Y - 1,)), dma((Y - 1,)),
            dma((Y - 1, R)), dma((Y - 1, R)),
            dma((R, H)), dma((R * H,)),
            dma, dma,
        ],
        compiler_params=pltpu.CompilerParams(collective_id=0, has_side_effects=True),
    )(section_input[0, 0], carried_grad[0, 0], hidden_grad[0, 0], saved_gate[0, 0], w_up[0])
    return passed.reshape(1, 1, rows, width), weight_grad.reshape(1, cols, hidden)


def solution(mesh):
    return jax.shard_map(
        body,
        mesh=mesh,
        in_specs=(
            P("section", "dp", "tensor", None),
            P("section", "dp", "tensor", None),
            P("section", "dp", None, "tensor"),
            P("section", "dp", None, "tensor"),
            P("section", "dp", "tensor"),
        ),
        out_specs=(P("section", "dp", "tensor", None), P("section", "dp", "tensor")),
        check_vma=False,
    )
```

```python
import functools

import jax
import jax.numpy as jnp
from jax import lax
from jax.experimental import pallas as pl
from jax.experimental.pallas import tpu as pltpu
from jax.sharding import PartitionSpec as P

MESH = pl.DeviceIdType.MESH
R = 4
H = 4
Y = 4
X_STEP = 1
CHUNKS = 2


def block_at(position, step):
    near = jnp.minimum(position, R - 1 - position)
    low = jnp.where((near == 1) & (step < 2), 1 - step, step)
    return jnp.where(position < 2, low, R - 1 - low)


def kernel(
    x_hbm, carried_hbm, grads_hbm, gates_hbm, w_hbm,
    passed, weight_hbm,
    x_in, carried, grads, gates, w, weight_grad, in_sems, out_sems,
    up, part, from_y, total, from_z, x, carry,
    up_send, up_recv, xz_send, xz_recv, xy_send, xy_recv,
    py_send, py_recv, pz_send, pz_recv, carry_send, carry_recv,
):
    section = lax.axis_index("section")
    sections = lax.axis_size("section")
    dp = lax.axis_index("dp")
    tensor = lax.axis_index("tensor")
    hi = tensor // Y
    y = lax.rem(tensor, Y)
    z = hi * R + dp
    tokens, hidden = grads.shape
    rows = x_in.shape[0]
    cols = w.shape[0]
    piece = tokens // CHUNKS

    def at(sec, r, h, yy):
        return {"section": sec, "dp": r, "tensor": h * Y + yy}

    def remote(src, dst, send, recv, device):
        return pltpu.make_async_remote_copy(
            src_ref=src, dst_ref=dst, send_sem=send, recv_sem=recv, device_id=device, device_id_type=MESH
        )

    barrier = pltpu.get_barrier_semaphore()

    def greet(k, _):
        other = lax.rem(z + k, R * H)
        pl.semaphore_signal(
            barrier, inc=1, device_id=at(section, lax.rem(other, R), other // R, y), device_id_type=MESH
        )
        return 0

    lax.fori_loop(1, R * H, greet, 0)
    for k in range(1, Y):
        pl.semaphore_signal(
            barrier, inc=1, device_id=at(section, dp, hi, lax.rem(y + k, Y)), device_id_type=MESH
        )

    @pl.when(section < sections - 1)
    def _():
        def greet_next(other, _):
            pl.semaphore_signal(
                barrier, inc=1, device_id=at(section + 1, lax.rem(other, R), other // R, y), device_id_type=MESH
            )
            return 0

        lax.fori_loop(0, R * H, greet_next, 0)

    loads = [
        pltpu.make_async_copy(src, dst, in_sems.at[i])
        for i, (src, dst) in enumerate(
            [(grads_hbm, grads), (gates_hbm, gates), (x_hbm, x_in), (carried_hbm, carried), (w_hbm, w)]
        )
    ]
    for load in loads:
        load.start()
    loads[0].wait()
    loads[1].wait()

    def activate(i, _):
        at_rows = pl.ds(pl.multiple_of(i * 64, 64), 64)
        gate = gates[at_rows, :].astype(jnp.float32)
        value = grads[at_rows, :].astype(jnp.float32) * gate * jax.nn.sigmoid(gate)
        up[dp, at_rows, :] = value.astype(jnp.bfloat16)
        return 0

    lax.fori_loop(0, tokens // 64, activate, 0)
    loads[2].wait()
    loads[3].wait()
    x[dp, hi, y] = x_in[:, pl.ds(pl.multiple_of(dp * cols, cols), cols)]

    pl.semaphore_wait(barrier, R * H - 1 + Y - 1 + R * H * jnp.minimum(section, 1))

    def up_copy(o, c, way):
        ref = up.at[o, pl.ds(c * piece, piece)]
        return remote(
            ref, ref, up_send.at[way, o, c], up_recv.at[o, c],
            at(section, jnp.clip(dp + (1 if way == 1 else -1), 0, R - 1), hi, y),
        )

    def to_right(o):
        return (dp < R - 1) & (o <= dp)

    def to_left(o):
        return (dp > 0) & (o >= dp)

    def pass_on(o, c):
        @pl.when(to_right(o))
        def _():
            up_copy(o, c, 1).start()

        @pl.when(to_left(o))
        def _():
            up_copy(o, c, 0).start()

    def carry_copy():
        return remote(carried, carry, carry_send, carry_recv, at(jnp.maximum(section - 1, 0), dp, hi, y))

    def part_copy(o, k):
        peer = lax.rem(y + k, Y)
        return remote(
            part.at[o, :, peer], from_y.at[k - 1, o], py_send.at[k - 1, o], py_recv.at[k - 1, o],
            at(section, dp, hi, peer),
        )

    def xz_copy(k):
        other = lax.rem(z + k, R * H)
        d = lax.rem(other, R)
        return remote(
            x_in.at[:, pl.ds(pl.multiple_of(d * cols, cols), cols)], x.at[dp, hi, y],
            xz_send.at[k], xz_recv.at[k], at(section, d, other // R, y),
        )

    def send_x(i, _):
        half = i // 2
        xz_copy(jnp.where(lax.rem(i, 2) == 0, half + 1, R * H - 1 - half)).start()
        return 0

    def xy_copy(k):
        mine = x.at[:, :, y]
        return remote(
            mine, mine, xy_send.at[k - 1], xy_recv.at[k - 1], at(section, dp, hi, lax.rem(y + k, Y))
        )

    def total_copy(o, h):
        return remote(
            total.at[o, h], from_z.at[z], pz_send.at[o, h], pz_recv.at[z],
            at(jnp.maximum(section - 1, 0), o, h, y),
        )

    def wait_x(k, _):
        xz_copy(k).wait_recv()
        return 0

    def add_up(step):
        o = block_at(dp, step)
        for k in range(1, Y):
            part_copy(o, k).wait_recv()
        for h in range(H):
            value = part[o, h, y].astype(jnp.float32)
            for k in range(1, Y):
                value = value + from_y[k - 1, o, h].astype(jnp.float32)
            total[o, h] = value.astype(jnp.bfloat16)

        @pl.when(section > 0)
        def _():
            for h in range(H):
                total_copy(o, h).start()

    def multiply(step, _):
        o = block_at(dp, step)
        for c in range(CHUNKS):

            @pl.when(step > 0)
            def _():
                up_copy(o, c, 0).wait_recv()
                pass_on(o, c)

        def tile(n, _):
            at_cols = pl.ds(pl.multiple_of(n * 256, 256), 256)
            out = lax.dot_general(
                up[o], w[at_cols, :], (((1,), (1,)), ((), ())), preferred_element_type=jnp.float32
            )
            part[o, :, :, :, at_cols] = out.astype(jnp.bfloat16).reshape(H, Y, rows, 256)
            return 0

        lax.fori_loop(0, cols // 256, tile, 0)
        for k in (1, 3, 2):
            part_copy(o, k).start()

        @pl.when(step > 0)
        def _():
            add_up(step - 1)

        @pl.when(step == X_STEP)
        def _():
            lax.fori_loop(1, R * H, wait_x, 0)
            for k in (1, 3, 2):
                xy_copy(k).start()

        return 0

    for c in range(CHUNKS):
        pass_on(dp, c)
    lax.fori_loop(0, R * H - 1, send_x, 0)

    @pl.when(section > 0)
    def _():
        carry_copy().start()

    loads[4].wait()
    lax.fori_loop(0, R, multiply, 0)
    add_up(R - 1)

    for k in (1, 3, 2):
        xy_copy(k).wait_recv()

    up_all = up.reshape(R * tokens, hidden)

    def store(n):
        at_rows = pl.ds(pl.multiple_of(n * 256, 256), 256)
        return pltpu.make_async_copy(weight_grad.at[at_rows], weight_hbm.at[at_rows], out_sems.at[n])

    def weight_tile(n, _):
        at_cols = pl.ds(pl.multiple_of(n * 256, 256), 256)
        xs = x[:, :, :, :, at_cols].reshape(R * tokens, 256)
        out = lax.dot_general(
            xs, up_all[...], (((0,), (0,)), ((), ())), preferred_element_type=jnp.float32
        )
        weight_grad[at_cols, :] = (out * (1.0 / R)).astype(jnp.bfloat16)
        store(n).start()
        return 0

    lax.fori_loop(0, cols // 256, weight_tile, 0)

    @pl.when(section < sections - 1)
    def _():
        carry_copy().wait_recv()

        def wait_total(other, _):
            remote(
                total.at[0, 0], from_z.at[other], pz_send.at[0, 0], pz_recv.at[other],
                at(jnp.maximum(section - 1, 0), dp, hi, y),
            ).wait_recv()
            return 0

        lax.fori_loop(0, R * H, wait_total, 0)
        for d in range(R):
            at_cols = pl.ds(d * cols, cols)
            value = from_z[d].astype(jnp.float32)
            for h in range(1, H):
                value = value + from_z[h * R + d].astype(jnp.float32)
            passed[:, at_cols] = (carry[:, at_cols].astype(jnp.float32) + value).astype(jnp.bfloat16)

    @pl.when(section == sections - 1)
    def _():
        passed[...] = jnp.zeros_like(passed)

    @pl.when(section > 0)
    def _():
        carry_copy().wait_send()
        for o in range(R):
            for h in range(H):
                total_copy(o, h).wait_send()

    def sent(o, _):
        for c in range(CHUNKS):

            @pl.when(to_right(o))
            def _():
                up_copy(o, c, 1).wait_send()

            @pl.when(to_left(o))
            def _():
                up_copy(o, c, 0).wait_send()

        for k in range(1, Y):
            part_copy(o, k).wait_send()
        return 0

    lax.fori_loop(0, R, sent, 0)

    def sent_x(k, _):
        xz_copy(k).wait_send()
        return 0

    lax.fori_loop(1, R * H, sent_x, 0)
    for k in range(1, Y):
        xy_copy(k).wait_send()
    for n in range(4):
        store(n).wait()


def body(section_input, carried_grad, hidden_grad, saved_gate, w_up):
    rows, width = section_input.shape[2:]
    tokens, hidden = hidden_grad.shape[2:]
    cols = w_up.shape[1]
    low = jnp.bfloat16
    dma = pltpu.SemaphoreType.DMA
    vmem = pl.BlockSpec(memory_space=pltpu.VMEM)
    hbm = pl.BlockSpec(memory_space=pl.ANY)
    passed, weight_grad = pl.pallas_call(
        kernel,
        out_shape=(jax.ShapeDtypeStruct((rows, width), low), jax.ShapeDtypeStruct((cols, hidden), low)),
        in_specs=[hbm] * 5,
        out_specs=(vmem, hbm),
        scratch_shapes=[
            pltpu.VMEM((rows, width), low),
            pltpu.VMEM((rows, width), low),
            pltpu.VMEM((tokens, hidden), low),
            pltpu.VMEM((tokens, hidden), low),
            pltpu.VMEM((cols, hidden), low),
            pltpu.VMEM((cols, hidden), low),
            dma((5,)), dma((4,)),
            pltpu.VMEM((R, tokens, hidden), low),
            pltpu.VMEM((R, H, Y, rows, cols), low),
            pltpu.VMEM((Y - 1, R, H, rows, cols), low),
            pltpu.VMEM((R, H, rows, cols), low),
            pltpu.VMEM((R * H, rows, cols), low),
            pltpu.VMEM((R, H, Y, rows, cols), low),
            pltpu.VMEM((rows, width), low),
            dma((2, R, CHUNKS)), dma((R, CHUNKS)),
            dma((R * H,)), dma((R * H,)),
            dma((Y - 1,)), dma((Y - 1,)),
            dma((Y - 1, R)), dma((Y - 1, R)),
            dma((R, H)), dma((R * H,)),
            dma, dma,
        ],
        compiler_params=pltpu.CompilerParams(collective_id=0, has_side_effects=True),
    )(section_input[0, 0], carried_grad[0, 0], hidden_grad[0, 0], saved_gate[0, 0], w_up[0])
    return passed.reshape(1, 1, rows, width), weight_grad.reshape(1, cols, hidden)


def solution(mesh):
    return jax.shard_map(
        body,
        mesh=mesh,
        in_specs=(
            P("section", "dp", "tensor", None),
            P("section", "dp", "tensor", None),
            P("section", "dp", None, "tensor"),
            P("section", "dp", None, "tensor"),
            P("section", "dp", "tensor"),
        ),
        out_specs=(P("section", "dp", "tensor", None), P("section", "dp", "tensor")),
        check_vma=False,
    )
```

```python
import functools

import jax
import jax.numpy as jnp
from jax import lax
from jax.experimental import pallas as pl
from jax.experimental.pallas import tpu as pltpu
from jax.sharding import PartitionSpec as P

MESH = pl.DeviceIdType.MESH
R = 4
H = 4
Y = 4
FAR = 7
CHUNKS = 2


def block_at(position, step):
    near = jnp.minimum(position, R - 1 - position)
    low = jnp.where((near == 1) & (step < 2), 1 - step, step)
    return jnp.where(position < 2, low, R - 1 - low)


def kernel(
    x_hbm, carried_hbm, grads_hbm, gates_hbm, w_hbm,
    passed, weight_hbm,
    x_in, carried, grads, gates, w, weight_grad, in_sems, out_sems,
    up, part, from_y, total, from_z, x, carry,
    up_send, up_recv, xz_send, xz_recv, xy_send, xy_recv,
    py_send, py_recv, pz_send, pz_recv, carry_send, carry_recv,
):
    section = lax.axis_index("section")
    sections = lax.axis_size("section")
    dp = lax.axis_index("dp")
    tensor = lax.axis_index("tensor")
    hi = tensor // Y
    y = lax.rem(tensor, Y)
    z = hi * R + dp
    tokens, hidden = grads.shape
    rows = x_in.shape[0]
    cols = w.shape[0]
    piece = tokens // CHUNKS

    def at(sec, r, h, yy):
        return {"section": sec, "dp": r, "tensor": h * Y + yy}

    def remote(src, dst, send, recv, device):
        return pltpu.make_async_remote_copy(
            src_ref=src, dst_ref=dst, send_sem=send, recv_sem=recv, device_id=device, device_id_type=MESH
        )

    barrier = pltpu.get_barrier_semaphore()

    def greet(k, _):
        other = lax.rem(z + k, R * H)
        pl.semaphore_signal(
            barrier, inc=1, device_id=at(section, lax.rem(other, R), other // R, y), device_id_type=MESH
        )
        return 0

    lax.fori_loop(1, R * H, greet, 0)
    for k in range(1, Y):
        pl.semaphore_signal(
            barrier, inc=1, device_id=at(section, dp, hi, lax.rem(y + k, Y)), device_id_type=MESH
        )

    @pl.when(section < sections - 1)
    def _():
        def greet_next(other, _):
            pl.semaphore_signal(
                barrier, inc=1, device_id=at(section + 1, lax.rem(other, R), other // R, y), device_id_type=MESH
            )
            return 0

        lax.fori_loop(0, R * H, greet_next, 0)

    loads = [
        pltpu.make_async_copy(src, dst, in_sems.at[i])
        for i, (src, dst) in enumerate(
            [(grads_hbm, grads), (gates_hbm, gates), (x_hbm, x_in), (carried_hbm, carried), (w_hbm, w)]
        )
    ]
    for load in loads:
        load.start()
    loads[0].wait()
    loads[1].wait()

    def activate(i, _):
        at_rows = pl.ds(pl.multiple_of(i * 64, 64), 64)
        gate = gates[at_rows, :].astype(jnp.float32)
        value = grads[at_rows, :].astype(jnp.float32) * gate * jax.nn.sigmoid(gate)
        up[dp, at_rows, :] = value.astype(jnp.bfloat16)
        return 0

    lax.fori_loop(0, tokens // 64, activate, 0)
    loads[2].wait()
    loads[3].wait()
    x[dp, hi, y] = x_in[:, pl.ds(pl.multiple_of(dp * cols, cols), cols)]

    pl.semaphore_wait(barrier, R * H - 1 + Y - 1 + R * H * jnp.minimum(section, 1))

    def up_copy(o, c, way):
        ref = up.at[o, pl.ds(c * piece, piece)]
        return remote(
            ref, ref, up_send.at[way, o, c], up_recv.at[o, c],
            at(section, jnp.clip(dp + (1 if way == 1 else -1), 0, R - 1), hi, y),
        )

    def to_right(o):
        return (dp < R - 1) & (o <= dp)

    def to_left(o):
        return (dp > 0) & (o >= dp)

    def pass_on(o, c):
        @pl.when(to_right(o))
        def _():
            up_copy(o, c, 1).start()

        @pl.when(to_left(o))
        def _():
            up_copy(o, c, 0).start()

    def carry_copy():
        return remote(carried, carry, carry_send, carry_recv, at(jnp.maximum(section - 1, 0), dp, hi, y))

    def part_copy(o, k):
        peer = lax.rem(y + k, Y)
        return remote(
            part.at[o, :, peer], from_y.at[k - 1, o], py_send.at[k - 1, o], py_recv.at[k - 1, o],
            at(section, dp, hi, peer),
        )

    def xz_copy(k):
        other = lax.rem(z + k, R * H)
        d = lax.rem(other, R)
        return remote(
            x_in.at[:, pl.ds(pl.multiple_of(d * cols, cols), cols)], x.at[dp, hi, y],
            xz_send.at[k], xz_recv.at[k], at(section, d, other // R, y),
        )

    def turn(i):
        half = i // 2
        return jnp.where(lax.rem(i, 2) == 0, half + 1, R * H - 1 - half)

    def send_x(i, _):
        xz_copy(turn(i)).start()
        return 0

    def xy_copy(k):
        mine = x.at[:, :, y]
        return remote(
            mine, mine, xy_send.at[k - 1], xy_recv.at[k - 1], at(section, dp, hi, lax.rem(y + k, Y))
        )

    def total_copy(o, h):
        return remote(
            total.at[o, h], from_z.at[z], pz_send.at[o, h], pz_recv.at[z],
            at(jnp.maximum(section - 1, 0), o, h, y),
        )

    def spread(source):
        mine = x.at[lax.rem(source, R), source // R, y]
        for k in (1, 3, 2):
            remote(
                mine, mine, xy_send.at[k - 1], xy_recv.at[k - 1], at(section, dp, hi, lax.rem(y + k, Y))
            ).start()

    def onward(source, k):
        step = jnp.where(k < R * H // 2, R, R * H - R)
        other = lax.rem(z + step, R * H)
        later = lax.rem(k + step, R * H)
        mine = x.at[lax.rem(source, R), source // R, y]
        return remote(
            mine, mine, xz_send.at[later], xz_recv.at[later], at(section, lax.rem(other, R), other // R, y)
        )

    def relay_x(i, _):
        k = turn(i)
        xz_copy(k).wait_recv()
        source = lax.rem(z + R * H - k, R * H)

        @pl.when(i < FAR)
        def _():
            onward(source, k).start()

        spread(source)
        return 0

    def add_up(step):
        o = block_at(dp, step)
        for k in range(1, Y):
            part_copy(o, k).wait_recv()
        for h in range(H):
            value = part[o, h, y].astype(jnp.float32)
            for k in range(1, Y):
                value = value + from_y[k - 1, o, h].astype(jnp.float32)
            total[o, h] = value.astype(jnp.bfloat16)

        @pl.when(section > 0)
        def _():
            for h in range(H):
                total_copy(o, h).start()

    def multiply(step, _):
        o = block_at(dp, step)
        for c in range(CHUNKS):

            @pl.when(step > 0)
            def _():
                up_copy(o, c, 0).wait_recv()
                pass_on(o, c)

        def tile(n, _):
            at_cols = pl.ds(pl.multiple_of(n * 256, 256), 256)
            out = lax.dot_general(
                up[o], w[at_cols, :], (((1,), (1,)), ((), ())), preferred_element_type=jnp.float32
            )
            part[o, :, :, :, at_cols] = out.astype(jnp.bfloat16).reshape(H, Y, rows, 256)
            return 0

        lax.fori_loop(0, cols // 256, tile, 0)
        for k in (1, 3, 2):
            part_copy(o, k).start()

        @pl.when(step > 0)
        def _():
            add_up(step - 1)

        @pl.when(step == 1)
        def _():
            lax.fori_loop(0, 8, relay_x, 0)

        @pl.when(step == 2)
        def _():
            lax.fori_loop(8, 15, relay_x, 0)

        return 0

    for c in range(CHUNKS):
        pass_on(dp, c)
    lax.fori_loop(0, R * H - 1 - FAR, send_x, 0)
    spread(z)

    @pl.when(section > 0)
    def _():
        carry_copy().start()

    loads[4].wait()
    lax.fori_loop(0, R, multiply, 0)
    add_up(R - 1)

    for k in (1, 3, 2):
        xy_copy(k).wait_recv()

    up_all = up.reshape(R * tokens, hidden)

    def store(n):
        at_rows = pl.ds(pl.multiple_of(n * 256, 256), 256)
        return pltpu.make_async_copy(weight_grad.at[at_rows], weight_hbm.at[at_rows], out_sems.at[n])

    def weight_tile(n, _):
        at_cols = pl.ds(pl.multiple_of(n * 256, 256), 256)
        xs = x[:, :, :, :, at_cols].reshape(R * tokens, 256)
        out = lax.dot_general(
            xs, up_all[...], (((0,), (0,)), ((), ())), preferred_element_type=jnp.float32
        )
        weight_grad[at_cols, :] = (out * (1.0 / R)).astype(jnp.bfloat16)
        store(n).start()
        return 0

    lax.fori_loop(0, cols // 256, weight_tile, 0)

    @pl.when(section < sections - 1)
    def _():
        carry_copy().wait_recv()

        def wait_total(other, _):
            remote(
                total.at[0, 0], from_z.at[other], pz_send.at[0, 0], pz_recv.at[other],
                at(jnp.maximum(section - 1, 0), dp, hi, y),
            ).wait_recv()
            return 0

        lax.fori_loop(0, R * H, wait_total, 0)
        for d in range(R):
            at_cols = pl.ds(d * cols, cols)
            value = from_z[d].astype(jnp.float32)
            for h in range(1, H):
                value = value + from_z[h * R + d].astype(jnp.float32)
            passed[:, at_cols] = (carry[:, at_cols].astype(jnp.float32) + value).astype(jnp.bfloat16)

    @pl.when(section == sections - 1)
    def _():
        passed[...] = jnp.zeros_like(passed)

    @pl.when(section > 0)
    def _():
        carry_copy().wait_send()
        for o in range(R):
            for h in range(H):
                total_copy(o, h).wait_send()

    def sent(o, _):
        for c in range(CHUNKS):

            @pl.when(to_right(o))
            def _():
                up_copy(o, c, 1).wait_send()

            @pl.when(to_left(o))
            def _():
                up_copy(o, c, 0).wait_send()

        for k in range(1, Y):
            part_copy(o, k).wait_send()
        return 0

    lax.fori_loop(0, R, sent, 0)

    def sent_x(k, _):
        xz_copy(k).wait_send()
        return 0

    lax.fori_loop(1, R * H, sent_x, 0)
    for k in range(1, Y):
        xy_copy(k).wait_send()
    for n in range(4):
        store(n).wait()


def body(section_input, carried_grad, hidden_grad, saved_gate, w_up):
    rows, width = section_input.shape[2:]
    tokens, hidden = hidden_grad.shape[2:]
    cols = w_up.shape[1]
    low = jnp.bfloat16
    dma = pltpu.SemaphoreType.DMA
    vmem = pl.BlockSpec(memory_space=pltpu.VMEM)
    hbm = pl.BlockSpec(memory_space=pl.ANY)
    passed, weight_grad = pl.pallas_call(
        kernel,
        out_shape=(jax.ShapeDtypeStruct((rows, width), low), jax.ShapeDtypeStruct((cols, hidden), low)),
        in_specs=[hbm] * 5,
        out_specs=(vmem, hbm),
        scratch_shapes=[
            pltpu.VMEM((rows, width), low),
            pltpu.VMEM((rows, width), low),
            pltpu.VMEM((tokens, hidden), low),
            pltpu.VMEM((tokens, hidden), low),
            pltpu.VMEM((cols, hidden), low),
            pltpu.VMEM((cols, hidden), low),
            dma((5,)), dma((4,)),
            pltpu.VMEM((R, tokens, hidden), low),
            pltpu.VMEM((R, H, Y, rows, cols), low),
            pltpu.VMEM((Y - 1, R, H, rows, cols), low),
            pltpu.VMEM((R, H, rows, cols), low),
            pltpu.VMEM((R * H, rows, cols), low),
            pltpu.VMEM((R, H, Y, rows, cols), low),
            pltpu.VMEM((rows, width), low),
            dma((2, R, CHUNKS)), dma((R, CHUNKS)),
            dma((R * H,)), dma((R * H,)),
            dma((Y - 1,)), dma((Y - 1,)),
            dma((Y - 1, R)), dma((Y - 1, R)),
            dma((R, H)), dma((R * H,)),
            dma, dma,
        ],
        compiler_params=pltpu.CompilerParams(collective_id=0, has_side_effects=True),
    )(section_input[0, 0], carried_grad[0, 0], hidden_grad[0, 0], saved_gate[0, 0], w_up[0])
    return passed.reshape(1, 1, rows, width), weight_grad.reshape(1, cols, hidden)


def solution(mesh):
    return jax.shard_map(
        body,
        mesh=mesh,
        in_specs=(
            P("section", "dp", "tensor", None),
            P("section", "dp", "tensor", None),
            P("section", "dp", None, "tensor"),
            P("section", "dp", None, "tensor"),
            P("section", "dp", "tensor"),
        ),
        out_specs=(P("section", "dp", "tensor", None), P("section", "dp", "tensor")),
        check_vma=False,
    )
```

```python
import functools

import jax
import jax.numpy as jnp
from jax import lax
from jax.experimental import pallas as pl
from jax.experimental.pallas import tpu as pltpu
from jax.sharding import PartitionSpec as P

MESH = pl.DeviceIdType.MESH
R = 4
H = 4
Y = 4
FAR = 7
CHUNKS = 4


def block_at(position, step):
    near = jnp.minimum(position, R - 1 - position)
    low = jnp.where((near == 1) & (step < 2), 1 - step, step)
    return jnp.where(position < 2, low, R - 1 - low)


def kernel(
    x_hbm, carried_hbm, grads_hbm, gates_hbm, w_hbm,
    passed, weight_hbm,
    x_in, carried, grads, gates, w, weight_grad, in_sems, out_sems,
    up, part, from_y, total, from_z, x, carry,
    up_send, up_recv, xz_send, xz_recv, xy_send, xy_recv,
    py_send, py_recv, pz_send, pz_recv, carry_send, carry_recv,
):
    section = lax.axis_index("section")
    sections = lax.axis_size("section")
    dp = lax.axis_index("dp")
    tensor = lax.axis_index("tensor")
    hi = tensor // Y
    y = lax.rem(tensor, Y)
    z = hi * R + dp
    tokens, hidden = grads.shape
    rows = x_in.shape[0]
    cols = w.shape[0]
    piece = tokens // CHUNKS

    def at(sec, r, h, yy):
        return {"section": sec, "dp": r, "tensor": h * Y + yy}

    def remote(src, dst, send, recv, device):
        return pltpu.make_async_remote_copy(
            src_ref=src, dst_ref=dst, send_sem=send, recv_sem=recv, device_id=device, device_id_type=MESH
        )

    barrier = pltpu.get_barrier_semaphore()

    def greet(k, _):
        other = lax.rem(z + k, R * H)
        pl.semaphore_signal(
            barrier, inc=1, device_id=at(section, lax.rem(other, R), other // R, y), device_id_type=MESH
        )
        return 0

    lax.fori_loop(1, R * H, greet, 0)
    for k in range(1, Y):
        pl.semaphore_signal(
            barrier, inc=1, device_id=at(section, dp, hi, lax.rem(y + k, Y)), device_id_type=MESH
        )

    @pl.when(section < sections - 1)
    def _():
        def greet_next(other, _):
            pl.semaphore_signal(
                barrier, inc=1, device_id=at(section + 1, lax.rem(other, R), other // R, y), device_id_type=MESH
            )
            return 0

        lax.fori_loop(0, R * H, greet_next, 0)

    loads = [
        pltpu.make_async_copy(src, dst, in_sems.at[i])
        for i, (src, dst) in enumerate(
            [(grads_hbm, grads), (gates_hbm, gates), (x_hbm, x_in), (carried_hbm, carried), (w_hbm, w)]
        )
    ]
    for load in loads:
        load.start()
    loads[0].wait()
    loads[1].wait()

    def activate(i, _):
        at_rows = pl.ds(pl.multiple_of(i * 64, 64), 64)
        gate = gates[at_rows, :].astype(jnp.float32)
        value = grads[at_rows, :].astype(jnp.float32) * gate * jax.nn.sigmoid(gate)
        up[dp, at_rows, :] = value.astype(jnp.bfloat16)
        return 0

    lax.fori_loop(0, tokens // 64, activate, 0)
    loads[2].wait()
    loads[3].wait()
    x[dp, hi, y] = x_in[:, pl.ds(pl.multiple_of(dp * cols, cols), cols)]

    pl.semaphore_wait(barrier, R * H - 1 + Y - 1 + R * H * jnp.minimum(section, 1))

    def up_copy(o, c, way):
        ref = up.at[o, pl.ds(c * piece, piece)]
        return remote(
            ref, ref, up_send.at[way, o, c], up_recv.at[o, c],
            at(section, jnp.clip(dp + (1 if way == 1 else -1), 0, R - 1), hi, y),
        )

    def to_right(o):
        return (dp < R - 1) & (o <= dp)

    def to_left(o):
        return (dp > 0) & (o >= dp)

    def pass_on(o, c):
        @pl.when(to_right(o))
        def _():
            up_copy(o, c, 1).start()

        @pl.when(to_left(o))
        def _():
            up_copy(o, c, 0).start()

    def carry_copy():
        return remote(carried, carry, carry_send, carry_recv, at(jnp.maximum(section - 1, 0), dp, hi, y))

    def part_copy(o, k):
        peer = lax.rem(y + k, Y)
        return remote(
            part.at[o, :, peer], from_y.at[k - 1, o], py_send.at[k - 1, o], py_recv.at[k - 1, o],
            at(section, dp, hi, peer),
        )

    def xz_copy(k):
        other = lax.rem(z + k, R * H)
        d = lax.rem(other, R)
        return remote(
            x_in.at[:, pl.ds(pl.multiple_of(d * cols, cols), cols)], x.at[dp, hi, y],
            xz_send.at[k], xz_recv.at[k], at(section, d, other // R, y),
        )

    def turn(i):
        half = i // 2
        return jnp.where(lax.rem(i, 2) == 0, half + 1, R * H - 1 - half)

    def send_x(i, _):
        xz_copy(turn(i)).start()
        return 0

    def xy_copy(k):
        mine = x.at[:, :, y]
        return remote(
            mine, mine, xy_send.at[k - 1], xy_recv.at[k - 1], at(section, dp, hi, lax.rem(y + k, Y))
        )

    def total_copy(o, h):
        return remote(
            total.at[o, h], from_z.at[z], pz_send.at[o, h], pz_recv.at[z],
            at(jnp.maximum(section - 1, 0), o, h, y),
        )

    def spread(source):
        mine = x.at[lax.rem(source, R), source // R, y]
        for k in (1, 3, 2):
            remote(
                mine, mine, xy_send.at[k - 1], xy_recv.at[k - 1], at(section, dp, hi, lax.rem(y + k, Y))
            ).start()

    def onward(source, k):
        step = jnp.where(k < R * H // 2, R, R * H - R)
        other = lax.rem(z + step, R * H)
        later = lax.rem(k + step, R * H)
        mine = x.at[lax.rem(source, R), source // R, y]
        return remote(
            mine, mine, xz_send.at[later], xz_recv.at[later], at(section, lax.rem(other, R), other // R, y)
        )

    def relay_x(i, _):
        k = turn(i)
        xz_copy(k).wait_recv()
        source = lax.rem(z + R * H - k, R * H)

        @pl.when(i < FAR)
        def _():
            onward(source, k).start()

        spread(source)
        return 0

    def add_up(step):
        o = block_at(dp, step)
        for k in range(1, Y):
            part_copy(o, k).wait_recv()
        for h in range(H):
            value = part[o, h, y].astype(jnp.float32)
            for k in range(1, Y):
                value = value + from_y[k - 1, o, h].astype(jnp.float32)
            total[o, h] = value.astype(jnp.bfloat16)

        @pl.when(section > 0)
        def _():
            for h in range(H):
                total_copy(o, h).start()

    def multiply(step, _):
        o = block_at(dp, step)
        for c in range(CHUNKS):

            @pl.when(step > 0)
            def _():
                up_copy(o, c, 0).wait_recv()
                pass_on(o, c)

        @pl.when(step > 0)
        def _():
            add_up(step - 1)

        def tile(n, _):
            at_cols = pl.ds(pl.multiple_of(n * 256, 256), 256)
            out = lax.dot_general(
                up[o], w[at_cols, :], (((1,), (1,)), ((), ())), preferred_element_type=jnp.float32
            )
            part[o, :, :, :, at_cols] = out.astype(jnp.bfloat16).reshape(H, Y, rows, 256)
            return 0

        lax.fori_loop(0, cols // 256, tile, 0)
        for k in (1, 3, 2):
            part_copy(o, k).start()

        @pl.when(step == 1)
        def _():
            lax.fori_loop(0, 8, relay_x, 0)

        @pl.when(step == 2)
        def _():
            lax.fori_loop(8, 15, relay_x, 0)

        return 0

    for c in range(CHUNKS):
        pass_on(dp, c)
    lax.fori_loop(0, R * H - 1 - FAR, send_x, 0)
    spread(z)

    @pl.when(section > 0)
    def _():
        carry_copy().start()

    loads[4].wait()
    lax.fori_loop(0, R, multiply, 0)
    add_up(R - 1)

    for k in (1, 3, 2):
        xy_copy(k).wait_recv()

    up_all = up.reshape(R * tokens, hidden)

    def store(n):
        at_rows = pl.ds(pl.multiple_of(n * 256, 256), 256)
        return pltpu.make_async_copy(weight_grad.at[at_rows], weight_hbm.at[at_rows], out_sems.at[n])

    def weight_tile(n, _):
        at_cols = pl.ds(pl.multiple_of(n * 256, 256), 256)
        xs = x[:, :, :, :, at_cols].reshape(R * tokens, 256)
        out = lax.dot_general(
            xs, up_all[...], (((0,), (0,)), ((), ())), preferred_element_type=jnp.float32
        )
        weight_grad[at_cols, :] = (out * (1.0 / R)).astype(jnp.bfloat16)
        store(n).start()
        return 0

    lax.fori_loop(0, cols // 256, weight_tile, 0)

    @pl.when(section < sections - 1)
    def _():
        carry_copy().wait_recv()

        def wait_total(other, _):
            remote(
                total.at[0, 0], from_z.at[other], pz_send.at[0, 0], pz_recv.at[other],
                at(jnp.maximum(section - 1, 0), dp, hi, y),
            ).wait_recv()
            return 0

        lax.fori_loop(0, R * H, wait_total, 0)
        for d in range(R):
            at_cols = pl.ds(d * cols, cols)
            value = from_z[d].astype(jnp.float32)
            for h in range(1, H):
                value = value + from_z[h * R + d].astype(jnp.float32)
            passed[:, at_cols] = (carry[:, at_cols].astype(jnp.float32) + value).astype(jnp.bfloat16)

    @pl.when(section == sections - 1)
    def _():
        passed[...] = jnp.zeros_like(passed)

    @pl.when(section > 0)
    def _():
        carry_copy().wait_send()
        for o in range(R):
            for h in range(H):
                total_copy(o, h).wait_send()

    def sent(o, _):
        for c in range(CHUNKS):

            @pl.when(to_right(o))
            def _():
                up_copy(o, c, 1).wait_send()

            @pl.when(to_left(o))
            def _():
                up_copy(o, c, 0).wait_send()

        for k in range(1, Y):
            part_copy(o, k).wait_send()
        return 0

    lax.fori_loop(0, R, sent, 0)

    def sent_x(k, _):
        xz_copy(k).wait_send()
        return 0

    lax.fori_loop(1, R * H, sent_x, 0)
    for k in range(1, Y):
        xy_copy(k).wait_send()
    for n in range(4):
        store(n).wait()


def body(section_input, carried_grad, hidden_grad, saved_gate, w_up):
    rows, width = section_input.shape[2:]
    tokens, hidden = hidden_grad.shape[2:]
    cols = w_up.shape[1]
    low = jnp.bfloat16
    dma = pltpu.SemaphoreType.DMA
    vmem = pl.BlockSpec(memory_space=pltpu.VMEM)
    hbm = pl.BlockSpec(memory_space=pl.ANY)
    passed, weight_grad = pl.pallas_call(
        kernel,
        out_shape=(jax.ShapeDtypeStruct((rows, width), low), jax.ShapeDtypeStruct((cols, hidden), low)),
        in_specs=[hbm] * 5,
        out_specs=(vmem, hbm),
        scratch_shapes=[
            pltpu.VMEM((rows, width), low),
            pltpu.VMEM((rows, width), low),
            pltpu.VMEM((tokens, hidden), low),
            pltpu.VMEM((tokens, hidden), low),
            pltpu.VMEM((cols, hidden), low),
            pltpu.VMEM((cols, hidden), low),
            dma((5,)), dma((4,)),
            pltpu.VMEM((R, tokens, hidden), low),
            pltpu.VMEM((R, H, Y, rows, cols), low),
            pltpu.VMEM((Y - 1, R, H, rows, cols), low),
            pltpu.VMEM((R, H, rows, cols), low),
            pltpu.VMEM((R * H, rows, cols), low),
            pltpu.VMEM((R, H, Y, rows, cols), low),
            pltpu.VMEM((rows, width), low),
            dma((2, R, CHUNKS)), dma((R, CHUNKS)),
            dma((R * H,)), dma((R * H,)),
            dma((Y - 1,)), dma((Y - 1,)),
            dma((Y - 1, R)), dma((Y - 1, R)),
            dma((R, H)), dma((R * H,)),
            dma, dma,
        ],
        compiler_params=pltpu.CompilerParams(collective_id=0, has_side_effects=True),
    )(section_input[0, 0], carried_grad[0, 0], hidden_grad[0, 0], saved_gate[0, 0], w_up[0])
    return passed.reshape(1, 1, rows, width), weight_grad.reshape(1, cols, hidden)


def solution(mesh):
    return jax.shard_map(
        body,
        mesh=mesh,
        in_specs=(
            P("section", "dp", "tensor", None),
            P("section", "dp", "tensor", None),
            P("section", "dp", None, "tensor"),
            P("section", "dp", None, "tensor"),
            P("section", "dp", "tensor"),
        ),
        out_specs=(P("section", "dp", "tensor", None), P("section", "dp", "tensor")),
        check_vma=False,
    )
```
